32 devices in a mesh: tm: 4 (over x, core), span: 8 (over z, y).
Axes of the slice: x: 2, y: 2, z: 4, core: 2. Of those that a mesh axis runs over, the one named last changes fastest.
Arguments:
- forcing: bfloat16 [128, 8, 16, 128], P('tm', 'span'), may hold values from -1.5 to 1.5
- iterate: bfloat16 [128, 8, 16, 128], P('tm', 'span'), may hold values from -1.5 to 1.5
- initial: bfloat16 [8, 16, 128], P('span'), may hold values from -1.5 to 1.5
- stiffness: bfloat16 [8, 128, 128], P('span'), may hold values from -0.5 to 0.5
- coupling: bfloat16 [8, 128, 128], P('span'), may hold values from -0.5 to 0.5
- pivots: bfloat16 [128, 8, 2, 128, 128], P('tm', 'span'), may hold values from -0.375 to 0.375
Outputs:
- updated: float32 [128, 8, 16, 128], P('tm', 'span')
The draws below stay inside these ranges and needn't reach their ends.
All inputs are finite; a program needn't handle non-finite values.
Results may differ from the reference program's by a relative error of at most 0.0003.
Values may be sent and summed in bfloat16 or wider, within the bound.
A program may use at most 320 MiB of HBM per device.

```python
import math
import jax
import jax.numpy as jnp
from jax import lax

DOF = 128
L = 128
RC = 16
NP = 8


def steps_of(stream_key, dims, cuts, smallest, largest):
    def one(dim, parts):
        steps = jax.random.uniform(jax.random.fold_in(jax.random.fold_in(stream_key, 6), dim), (parts,), jnp.float32, smallest / len(cuts), largest / len(cuts))
        return jnp.repeat(jnp.exp(steps), dims[dim] // parts).reshape((-1,) + (1,) * (len(dims) - dim - 1))

    gain = one(*cuts[0])
    for cut in cuts[1:]:
        gain = gain * one(*cut)
    return gain


def normal_values(own_key, dims, spread, limit, shards=(), kind=jnp.bfloat16):
    factor_of = steps_of(own_key, dims, shards, -0.22, 0.18) if shards else 1.0
    entries = jax.random.normal(own_key, dims, jnp.float32) * spread * factor_of
    return jnp.minimum(jnp.maximum(entries, -limit), limit).astype(kind)


def setup_inputs(seed: int = 0) -> dict:
    keys = jax.random.split(jax.random.key(seed), 7)
    forcing = normal_values(keys[0], (L, NP, RC, DOF), 0.25, 1.5, ((0, 4), (1, 8)))
    iterate = normal_values(keys[1], (L, NP, RC, DOF), 0.25, 1.5, ((0, 4), (1, 8)))
    initial = normal_values(keys[2], (NP, RC, DOF), 0.25, 1.5, ((0, 8),))
    stiffness = normal_values(keys[3], (NP, DOF, DOF), DOF ** -0.5, 0.5, ((0, 8),))
    coupling = normal_values(keys[4], (NP, DOF, DOF), DOF ** -0.5, 0.5, ((0, 8),))
    pivots = normal_values(keys[5], (L, NP, 2, DOF, DOF), (DOF * 7 // 3) ** -0.5, 0.375, ((0, 4), (1, 8)))
    return dict(forcing=forcing, iterate=iterate, initial=initial, stiffness=stiffness, coupling=coupling, pivots=pivots)


PRECISE = lax.Precision.HIGHEST


def phase_table(row_ids, col_ids, total):
    turned = (row_ids[:, None] * col_ids[None, :]) % total
    angle = turned.astype(jnp.float32) * (2.0 * math.pi / total)
    return jnp.cos(angle), jnp.sin(angle)


def complex_product(left_real, left_imag, right_real, right_imag):
    form = "kcd,kde->kce"
    real_part = jnp.einsum(form, left_real, right_real, precision=PRECISE) - jnp.einsum(form, left_imag, right_imag, precision=PRECISE)
    imag_part = jnp.einsum(form, left_real, right_imag, precision=PRECISE) + jnp.einsum(form, left_imag, right_real, precision=PRECISE)
    return real_part, imag_part


def sweep_forward(spec_real, spec_imag, pivots, bonds, carry_real, carry_imag):
    count = spec_real.shape[1]

    def advance(plane_at, state):
        out_real, out_imag, into_real, into_imag = state
        pivot_now = lax.dynamic_index_in_dim(pivots, plane_at, 1, keepdims=False).astype(jnp.float32)
        bond = lax.dynamic_index_in_dim(bonds, plane_at, 0, keepdims=False)
        given_real = lax.dynamic_index_in_dim(spec_real, plane_at, 1, keepdims=False) - into_real
        given_imag = lax.dynamic_index_in_dim(spec_imag, plane_at, 1, keepdims=False) - into_imag
        pivot_real, pivot_imag = complex_product(given_real, given_imag, pivot_now[:, 0], pivot_now[:, 1])
        next_real = jnp.einsum("kcd,de->kce", pivot_real, bond, precision=PRECISE)
        next_imag = jnp.einsum("kcd,de->kce", pivot_imag, bond, precision=PRECISE)
        out_real = lax.dynamic_update_index_in_dim(out_real, pivot_real, plane_at, 1)
        out_imag = lax.dynamic_update_index_in_dim(out_imag, pivot_imag, plane_at, 1)
        return out_real, out_imag, next_real, next_imag

    start = (jnp.zeros_like(spec_real), jnp.zeros_like(spec_imag), carry_real, carry_imag)
    return lax.fori_loop(0, count, advance, start)


def sweep_backward(piv_real, piv_imag, pivots, bonds, carry_real, carry_imag):
    count = piv_real.shape[1]

    def retreat(step_at, state):
        out_real, out_imag, above_real, above_imag = state
        plane_at = count - 1 - step_at
        pivot_now = lax.dynamic_index_in_dim(pivots, plane_at, 1, keepdims=False).astype(jnp.float32)
        bond = lax.dynamic_index_in_dim(bonds, plane_at, 0, keepdims=False)
        bond_real = jnp.einsum("kce,de->kcd", above_real, bond, precision=PRECISE)
        bond_imag = jnp.einsum("kce,de->kcd", above_imag, bond, precision=PRECISE)
        mixed_real, mixed_imag = complex_product(bond_real, bond_imag, pivot_now[:, 0], pivot_now[:, 1])
        solved_real = lax.dynamic_index_in_dim(piv_real, plane_at, 1, keepdims=False) - mixed_real
        solved_imag = lax.dynamic_index_in_dim(piv_imag, plane_at, 1, keepdims=False) - mixed_imag
        out_real = lax.dynamic_update_index_in_dim(out_real, solved_real, plane_at, 1)
        out_imag = lax.dynamic_update_index_in_dim(out_imag, solved_imag, plane_at, 1)
        return out_real, out_imag, solved_real, solved_imag

    start = (jnp.zeros_like(piv_real), jnp.zeros_like(piv_imag), carry_real, carry_imag)
    return lax.fori_loop(0, count, retreat, start)


def reference(forcing, iterate, initial, stiffness, coupling, pivots):
    steps_all = iterate.shape[0]
    it_wide = iterate.astype(jnp.float32)
    prior_state = jnp.concatenate([initial[None], iterate[:-1]], 0)
    bonds = coupling.astype(jnp.float32)
    own_term = jnp.einsum("njcd,jde->njce", it_wide, stiffness.astype(jnp.float32))
    below = jnp.einsum("njcd,jde->njce", it_wide[:, :-1], bonds[:-1])
    above = jnp.einsum("njce,jde->njcd", it_wide[:, 1:], bonds[:-1])
    empty_plane = jnp.zeros_like(it_wide[:, :1])
    below = jnp.concatenate([empty_plane, below], 1)
    above = jnp.concatenate([above, empty_plane], 1)
    resid = forcing.astype(jnp.float32) - it_wide + prior_state.astype(jnp.float32) - (own_term + below + above)
    step_ids = jnp.arange(steps_all, dtype=jnp.int32)
    gamma = jnp.float32(0.5) ** (step_ids.astype(jnp.float32) / steps_all)
    scaled = resid * gamma[:, None, None, None]
    cosine, sine_table = phase_table(step_ids, step_ids, steps_all)
    spec_real = jnp.tensordot(cosine, scaled, axes=1, precision=PRECISE)
    spec_imag = -jnp.tensordot(sine_table, scaled, axes=1, precision=PRECISE)
    zero_vec = jnp.zeros_like(spec_real[:, 0])
    swept = sweep_forward(spec_real, spec_imag, pivots, bonds, zero_vec, zero_vec)
    solved = sweep_backward(swept[0], swept[1], pivots, bonds, zero_vec, zero_vec)
    correction = (jnp.tensordot(cosine, solved[0], axes=1, precision=PRECISE) - jnp.tensordot(sine_table, solved[1], axes=1, precision=PRECISE)) * (1.0 / steps_all)
    return it_wide + correction / gamma[:, None, None, None]
```

```python
import functools
import math

import jax
import jax.numpy as jnp
import numpy as np
from jax import lax
from jax.experimental import pallas as pl
from jax.experimental.pallas import tpu as pltpu
from jax.sharding import PartitionSpec as P

MESH = pl.DeviceIdType.MESH
F32 = jnp.float32
BF16 = jnp.bfloat16


def split(value):
    high = value.astype(BF16)
    low = (value - high.astype(F32)).astype(BF16)
    return high, low


def dot(a, b):
    return jnp.dot(a, b, preferred_element_type=F32)


def tables(total, blocks):
    ids = np.arange(total)
    theta = 2.0 * math.pi / total * ((ids[:, None] * ids[None, :]) % total)
    gamma = 0.5 ** (ids / total)
    here = total // blocks

    def three(table):
        high = table.astype(np.float32).astype(jnp.bfloat16)
        low = (table - high.astype(np.float64)).astype(np.float32).astype(jnp.bfloat16)
        return np.concatenate([high, high, low], -1)

    cosine = (np.cos(theta) * gamma).reshape(blocks, here, total)
    sine = (-np.sin(theta) * gamma).reshape(blocks, here, total)
    forward = three(np.concatenate([cosine, sine], 1))
    back = 1.0 / (total * gamma[:, None])
    cosine = (np.cos(theta) * back).reshape(total, blocks, here).transpose(1, 0, 2)
    sine = (-np.sin(theta) * back).reshape(total, blocks, here).transpose(1, 0, 2)
    inverse = three(np.concatenate([cosine, sine], 2))
    return forward, inverse


def kernel(
    n_tm, n_sp, chunks, cases, forcing, iterate, initial, stiff, coup, pivots, tf, ti, out,
    it_below, it_above, c_below, prior0, gath, weights, c2, ct2, spec, pv, q_in, q_out, x_in, x_out,
    contrib, rs1, rs2,
    nb_send, nb_recv, ag_send, ag_recv, f_send, f_recv, b_send, b_recv,
    r1_send, r1_recv, r2_send, r2_recv,
):
    tm, sp = lax.axis_index("tm"), lax.axis_index("span")
    rows, dof = iterate.shape
    steps = rows // cases
    total = steps * n_tm
    per = steps // chunks
    n_x = n_tm // 2
    core, x = tm % 2, tm // 2
    sib = 2 * x + 1 - core
    last = n_sp - 1
    has_below, has_above = sp > 0, sp < last

    def copy(src, dst, send, recv, **where):
        return pltpu.make_async_remote_copy(
            src_ref=src, dst_ref=dst, send_sem=send, recv_sem=recv, device_id=where, device_id_type=MESH
        )

    def block(b):
        return pl.ds(pl.multiple_of(b * rows, rows), rows)

    barrier = pltpu.get_barrier_semaphore()
    for i in range(1, n_tm):
        pl.semaphore_signal(barrier, inc=1, device_id={"tm": (tm + i) % n_tm}, device_id_type=MESH)

    @pl.when(has_below)
    def _():
        pl.semaphore_signal(barrier, inc=1, device_id={"span": sp - 1}, device_id_type=MESH)

    @pl.when(has_above)
    def _():
        pl.semaphore_signal(barrier, inc=1, device_id={"span": sp + 1}, device_id_type=MESH)

    pl.semaphore_wait(
        barrier, n_tm - 1 + has_below.astype(jnp.int32) + has_above.astype(jnp.int32)
    )

    to_up = copy(iterate, it_below, nb_send.at[0], nb_recv.at[0], span=sp + 1)
    to_down = copy(iterate, it_above, nb_send.at[1], nb_recv.at[1], span=sp - 1)
    c_up = copy(coup, c_below, nb_send.at[2], nb_recv.at[2], span=sp + 1)
    to_next = copy(
        iterate.at[pl.ds(rows - cases, cases)], prior0, nb_send.at[3], nb_recv.at[3], tm=tm + 1
    )

    @pl.when(tm < n_tm - 1)
    def _():
        to_next.start()

    @pl.when(has_above)
    def _():
        to_up.start()
        c_up.start()

    @pl.when(has_below)
    def _():
        to_down.start()

    mine = block(tm)
    it_wide = iterate[...].astype(F32)
    own = forcing[...].astype(F32) - it_wide - dot(iterate[...], stiff[...])
    own = own + jnp.concatenate([jnp.zeros((cases, dof), F32), it_wide[: rows - cases]], 0)
    gath[mine] = own
    first = pl.ds(pl.multiple_of(tm * rows, rows), cases)

    zero = jnp.zeros((dof, dof), BF16)
    bond = coup[...]
    bond_t = bond.astype(F32).T.astype(BF16)
    for ref, value in ((c2, bond), (ct2, bond_t)):
        ref[:dof, :dof] = value
        ref[dof:, dof:] = value
        ref[:dof, dof:] = zero
        ref[dof:, :dof] = zero

    def build(k, carry):
        real, imag = pivots[k, 0], pivots[k, 1]
        weights[k, :dof, :dof] = real
        weights[k, dof:, dof:] = real
        weights[k, :dof, dof:] = imag
        weights[k, dof:, :dof] = -imag
        return carry

    @pl.when(tm == 0)
    def _():
        gath[first] = gath[first] + initial[...].astype(F32)

    @pl.when(tm > 0)
    def _():
        to_next.wait_recv()
        gath[first] = gath[first] + prior0[...].astype(F32)

    @pl.when(has_above)
    def _():
        to_down.wait_recv()
        gath[mine] = gath[mine] - dot(it_above[...], ct2[:dof, :dof])

    @pl.when(has_below)
    def _():
        to_up.wait_recv()
        c_up.wait_recv()
        gath[mine] = gath[mine] - dot(it_below[...], c_below[...])

    def send_block(b, slot, peer):
        at = block(b)
        return copy(gath.at[at], gath.at[at], ag_send.at[slot], ag_recv.at[b], tm=peer)

    for i in range(1, n_x):
        send_block(tm, i, 2 * ((x + i) % n_x) + core).start()
    send_block(tm, 0, sib).start()
    lax.fori_loop(0, steps, build, 0)

    @pl.when(sp == 0)
    def _():
        q_in[...] = jnp.zeros_like(q_in)

    for i in range(1, n_x):
        b = 2 * ((x + n_x - i) % n_x) + core
        send_block(b, 0, sib).wait_recv()
        send_block(b, n_x + i, sib).start()
    for i in range(n_x):
        send_block(2 * ((x + n_x - i) % n_x) + 1 - core, 0, sib).wait_recv()

    forward = tf[tm]
    for case in range(0, cases, 2):
        value = jnp.concatenate(
            [gath[pl.ds(case + i, total, stride=cases), :] for i in range(2)], 1
        )
        high, low = split(value)
        result = dot(forward, jnp.concatenate([high, low, high], 0))
        for i in range(2):
            part = result[:, i * dof : (i + 1) * dof]
            spec[0, pl.ds(case + i, steps, stride=cases), :] = part[:steps]
            spec[1, pl.ds(case + i, steps, stride=cases), :] = part[steps:]

    size = per * cases

    def at_chunk(c):
        return pl.ds(pl.multiple_of(c * size, size), size)

    def f_copy(c):
        at = at_chunk(c)
        return copy(q_out.at[:, at], q_in.at[:, at], f_send.at[c], f_recv.at[c], span=sp + 1)

    def b_copy(c):
        at = at_chunk(c)
        return copy(x_out.at[:, at], x_in.at[:, at], b_send.at[c], b_recv.at[c], span=sp - 1)

    def wide(ref, at):
        return jnp.concatenate([ref[0, at, :], ref[1, at, :]], 1)

    def put(ref, at, value):
        ref[0, at, :] = value[:, :dof]
        ref[1, at, :] = value[:, dof:]

    def times_pivots(value, c):
        high, low = split(value)
        parts = []
        for f in range(per):
            at = slice(f * cases, (f + 1) * cases)
            both = dot(jnp.concatenate([high[at], low[at]], 0), weights[c * per + f])
            parts.append(both[:cases] + both[cases:])
        return jnp.concatenate(parts, 0)

    def times_bond(value, ref):
        both = dot(jnp.concatenate(split(value), 0), ref[...])
        return both[:size] + both[size:]

    def up(c):
        at = at_chunk(c)

        @pl.when(has_below)
        def _():
            f_copy(c).wait_recv()

        pivoted = times_pivots(wide(spec, at) - wide(q_in, at), c)

        @pl.when(has_above)
        def _():
            put(q_out, at, times_bond(pivoted, c2))
            f_copy(c).start()
            put(pv, at, pivoted)

        @pl.when(sp == last)
        def _():
            put(x_out, at, pivoted)
            b_copy(c).start()

    def down(c):
        at = at_chunk(c)
        b_copy(c).wait_recv()
        put(x_out, at, wide(pv, at) - times_pivots(times_bond(wide(x_in, at), ct2), c))

        @pl.when(has_below)
        def _():
            b_copy(c).start()

    lag = jnp.minimum(chunks, 3 * (last - sp))

    def turn(t, carry):
        @pl.when(t < chunks)
        def _():
            up(t)

        @pl.when(has_above & (t >= lag) & (t < lag + chunks))
        def _():
            down(t - lag)

        return carry

    lax.fori_loop(0, 2 * chunks, turn, 0)

    inverse = ti[tm]
    for case in range(0, cases, 2):
        value = jnp.concatenate(
            [
                jnp.concatenate(
                    [x_out[p, pl.ds(case + i, steps, stride=cases), :] for p in range(2)], 0
                )
                for i in range(2)
            ],
            1,
        )
        high, low = split(value)
        result = dot(inverse, jnp.concatenate([high, low, high], 0))
        for i in range(2):
            contrib[pl.ds(case + i, total, stride=cases), :] = result[:, i * dof : (i + 1) * dof]

    def r1_copy(i):
        there = (x + i) % n_x
        return copy(
            contrib.at[block(2 * there + 1 - core)], rs1.at[i], r1_send.at[i], r1_recv.at[i], tm=sib
        )

    def r2_copy(i):
        there = (x + i) % n_x
        return copy(
            contrib.at[block(2 * there + core)], rs2.at[i], r2_send.at[i], r2_recv.at[i],
            tm=2 * there + core,
        )

    order = list(range(1, n_x)) + [0]
    for i in order:
        r1_copy(i).start()
    for i in order:
        r1_copy(i).wait_recv()
        at = block(2 * ((x + i) % n_x) + core)
        contrib[at] = contrib[at] + rs1[i]
        if i:
            r2_copy(i).start()
    result = contrib[mine] + iterate[...].astype(F32)
    for i in range(1, n_x):
        r2_copy(i).wait_recv()
        result = result + rs2[i]
    out[...] = result

    @pl.when(tm < n_tm - 1)
    def _():
        to_next.wait_send()

    @pl.when(has_above)
    def _():
        to_up.wait_send()
        c_up.wait_send()

    @pl.when(has_below)
    def _():
        to_down.wait_send()

    for slot in range(2 * n_x):
        if slot != n_x:
            send_block(tm, slot, sib).wait_send()

    def drain(c, carry):
        @pl.when(has_above)
        def _():
            f_copy(c).wait_send()

        @pl.when(has_below)
        def _():
            b_copy(c).wait_send()

        return carry

    lax.fori_loop(0, chunks, drain, 0)
    for i in range(n_x):
        r1_copy(i).wait_send()
    for i in range(1, n_x):
        r2_copy(i).wait_send()


def on_device(n_tm, n_sp, forcing, iterate, initial, stiffness, coupling, pivots):
    steps, planes, cases, dof = forcing.shape
    assert planes == 1 and n_tm % 2 == 0 and n_sp > 1
    rows, total, n_x = steps * cases, steps * n_tm, n_tm // 2
    chunks = math.gcd(steps, 8)
    forward, inverse = tables(total, n_tm)
    state = pltpu.VMEM((2, rows, dof), F32)
    dma = pltpu.SemaphoreType.DMA
    vmem = pl.BlockSpec(memory_space=pltpu.VMEM)
    result = pl.pallas_call(
        functools.partial(kernel, n_tm, n_sp, chunks, cases),
        out_shape=jax.ShapeDtypeStruct((rows, dof), F32),
        in_specs=[vmem] * 8,
        out_specs=vmem,
        scratch_shapes=[
            pltpu.VMEM((rows, dof), BF16),
            pltpu.VMEM((rows, dof), BF16),
            pltpu.VMEM((dof, dof), BF16),
            pltpu.VMEM((cases, dof), BF16),
            pltpu.VMEM((total * cases, dof), F32),
            pltpu.VMEM((steps, 2 * dof, 2 * dof), BF16),
            pltpu.VMEM((2 * dof, 2 * dof), BF16),
            pltpu.VMEM((2 * dof, 2 * dof), BF16),
            state, state, state, state, state, state,
            pltpu.VMEM((total * cases, dof), F32),
            pltpu.VMEM((n_x, rows, dof), F32),
            pltpu.VMEM((n_x, rows, dof), F32),
            dma((4,)), dma((4,)), dma((2 * n_x,)), dma((n_tm,)),
            dma((chunks,)), dma((chunks,)), dma((chunks,)), dma((chunks,)),
            dma((n_x,)), dma((n_x,)), dma((n_x,)), dma((n_x,)),
        ],
        compiler_params=pltpu.CompilerParams(
            collective_id=0, has_side_effects=True, vmem_limit_bytes=48 * 2**20
        ),
    )(
        forcing.reshape(rows, dof),
        iterate.reshape(rows, dof),
        initial.reshape(cases, dof),
        stiffness.reshape(dof, dof),
        coupling.reshape(dof, dof),
        pivots.reshape(steps, 2, dof, dof),
        jnp.asarray(forward),
        jnp.asarray(inverse),
    )
    return result.reshape(steps, 1, cases, dof)


def solution(mesh):
    return jax.shard_map(
        functools.partial(on_device, mesh.shape["tm"], mesh.shape["span"]),
        mesh=mesh,
        in_specs=(
            P("tm", "span", None, None),
            P("tm", "span", None, None),
            P("span", None, None),
            P("span", None, None),
            P("span", None, None),
            P("tm", "span", None, None, None),
        ),
        out_specs=P("tm", "span", None, None),
        check_vma=False,
    )
```

```python
import functools
import math

import jax
import jax.numpy as jnp
import numpy as np
from jax import lax
from jax.experimental import pallas as pl
from jax.experimental.pallas import tpu as pltpu
from jax.sharding import PartitionSpec as P

MESH = pl.DeviceIdType.MESH
F32 = jnp.float32
CHUNKS = 4
LEAD = 4
BF16 = jnp.bfloat16


def split(value):
    high = value.astype(BF16)
    low = (value - high.astype(F32)).astype(BF16)
    return high, low


def dot(a, b):
    return jnp.dot(a, b, preferred_element_type=F32)


def tables(total, blocks):
    ids = np.arange(total)
    theta = 2.0 * math.pi / total * ((ids[:, None] * ids[None, :]) % total)
    gamma = 0.5 ** (ids / total)
    here = total // blocks

    def three(table):
        high = table.astype(np.float32).astype(jnp.bfloat16)
        low = (table - high.astype(np.float64)).astype(np.float32).astype(jnp.bfloat16)
        return np.concatenate([high, high, low], -1)

    half = here // 2
    cosine = (np.cos(theta) * gamma).reshape(blocks, 2, half, total)
    sine = (-np.sin(theta) * gamma).reshape(blocks, 2, half, total)
    forward = three(np.concatenate([cosine, sine], 2))
    back = 1.0 / (total * gamma[:, None])
    cosine = (np.cos(theta) * back).reshape(total, blocks, 2, half).transpose(1, 2, 0, 3)
    sine = (-np.sin(theta) * back).reshape(total, blocks, 2, half).transpose(1, 2, 0, 3)
    inverse = three(np.concatenate([cosine, sine], 3))
    return forward, inverse


def kernel(
    n_tm, n_sp, chunks, lead, cases, forcing_hbm, iterate_hbm, initial_hbm, stiff_hbm, coup_hbm,
    pivots_hbm, tf_hbm, ti_hbm, out,
    forcing, iterate, initial, stiff, coup, pivots, tf, ti,
    it_below, it_above, c_below, c_above, prior0, gath, weights, c2, ct2,
    spec, spec_out, pv, q_in, q_out, x_in, solved, other, contrib, rs1, rs2,
    ld, nb_send, nb_recv, p_send, p_recv, ag_send, ag_recv, s_send, s_recv,
    f_send, f_recv, b_send, b_recv, e_send, e_recv, r1_send, r1_recv, r2_send, r2_recv,
):
    tm, sp = lax.axis_index("tm"), lax.axis_index("span")
    rows, dof = iterate.shape
    steps = rows // cases
    total = steps * n_tm
    half = steps // 2
    per = half // chunks
    size = per * cases
    y = sp % 2
    peer = sp + 1 - 2 * y
    n_x = n_tm // 2
    core, x = tm % 2, tm // 2
    sib = 2 * x + 1 - core
    last = n_sp - 1
    has_below, has_above = sp > 0, sp < last
    pair_below, pair_above = sp > 1, sp < last - 1

    def copy(src, dst, send, recv, **where):
        return pltpu.make_async_remote_copy(
            src_ref=src, dst_ref=dst, send_sem=send, recv_sem=recv, device_id=where, device_id_type=MESH
        )

    loads = [
        pltpu.make_async_copy(src, dst, ld.at[i])
        for i, (src, dst) in enumerate(
            (
                (iterate_hbm, iterate),
                (stiff_hbm, stiff),
                (forcing_hbm, forcing),
                (initial_hbm, initial),
                (coup_hbm, coup),
                (tf_hbm.at[tm], tf),
                (ti_hbm.at[tm], ti),
                (pivots_hbm.at[pl.ds(y * half, half)], pivots.at[y]),
            )
        )
    ]
    for load in loads:
        load.start()

    def block(b):
        return pl.ds(pl.multiple_of(b * rows, rows), rows)

    barrier = pltpu.get_barrier_semaphore()
    for i in range(1, n_tm):
        pl.semaphore_signal(barrier, inc=1, device_id={"tm": (tm + i) % n_tm}, device_id_type=MESH)

    @pl.when(has_below)
    def _():
        pl.semaphore_signal(barrier, inc=1, device_id={"span": sp - 1}, device_id_type=MESH)

    @pl.when(has_above)
    def _():
        pl.semaphore_signal(barrier, inc=1, device_id={"span": sp + 1}, device_id_type=MESH)

    @pl.when(pair_below)
    def _():
        pl.semaphore_signal(barrier, inc=1, device_id={"span": sp - 2}, device_id_type=MESH)

    @pl.when(pair_above)
    def _():
        pl.semaphore_signal(barrier, inc=1, device_id={"span": sp + 2}, device_id_type=MESH)

    pl.semaphore_wait(
        barrier,
        n_tm - 1 + sum(t.astype(jnp.int32) for t in (has_below, has_above, pair_below, pair_above)),
    )

    to_up = copy(iterate_hbm, it_below, nb_send.at[0], nb_recv.at[0], span=sp + 1)
    to_down = copy(iterate_hbm, it_above, nb_send.at[1], nb_recv.at[1], span=sp - 1)
    c_up = copy(coup_hbm, c_below, nb_send.at[2], nb_recv.at[2], span=sp + 1)
    c_down = copy(coup_hbm, c_above, nb_send.at[4], nb_recv.at[4], span=sp - 1)
    to_next = copy(
        iterate_hbm.at[pl.ds(rows - cases, cases)], prior0, nb_send.at[3], nb_recv.at[3], tm=tm + 1
    )

    def p_copy(c):
        return copy(
            pivots_hbm.at[pl.ds((1 - y) * half + c * per, per)], pivots.at[y, pl.ds(c * per, per)],
            p_send.at[c], p_recv.at[c], span=peer,
        )

    @pl.when(tm < n_tm - 1)
    def _():
        to_next.start()

    @pl.when(has_above)
    def _():
        to_up.start()
        c_up.start()

    @pl.when(has_below)
    def _():
        to_down.start()

    @pl.when(y == 1)
    def _():
        c_down.start()

    for c in range(chunks):
        p_copy(c).start()

    mine = block(tm)
    for load in loads[:5]:
        load.wait()
    it_wide = iterate[...].astype(F32)
    own = forcing[...].astype(F32) - it_wide - dot(iterate[...], stiff[...])
    own = own + jnp.concatenate([jnp.zeros((cases, dof), F32), it_wide[: rows - cases]], 0)
    gath[mine] = own
    first = pl.ds(pl.multiple_of(tm * rows, rows), cases)

    def build(p, k):
        real, imag = pivots[p, k, 0], pivots[p, k, 1]
        weights[p, k, :dof, :dof] = real
        weights[p, k, dof:, dof:] = real
        weights[p, k, :dof, dof:] = imag
        weights[p, k, dof:, :dof] = -imag

    def build_own(k, carry):
        build(y, k)
        return carry

    @pl.when(tm == 0)
    def _():
        gath[first] = gath[first] + initial[...].astype(F32)

    @pl.when(tm > 0)
    def _():
        to_next.wait_recv()
        gath[first] = gath[first] + prior0[...].astype(F32)

    @pl.when(has_above)
    def _():
        to_down.wait_recv()
        gath[mine] = gath[mine] - lax.dot_general(
            it_above[...], coup[...], (((1,), (1,)), ((), ())), preferred_element_type=F32
        )

    @pl.when(has_below)
    def _():
        to_up.wait_recv()
        c_up.wait_recv()
        gath[mine] = gath[mine] - dot(it_below[...], c_below[...])

    def send_block(b, slot, peer):
        at = block(b)
        return copy(gath.at[at], gath.at[at], ag_send.at[slot], ag_recv.at[b], tm=peer)

    for i in range(1, n_x):
        send_block(tm, i, 2 * ((x + i) % n_x) + core).start()
    send_block(tm, 0, sib).start()

    @pl.when(y == 1)
    def _():
        c_down.wait_send()

    @pl.when(y == 0)
    def _():
        c_down.wait_recv()

    zero = jnp.zeros((dof, dof), BF16)
    bonds = (
        jnp.where(y == 0, coup[...], c_below[...]), jnp.where(y == 0, c_above[...], coup[...])
    )
    for p in range(2):
        for ref, value in ((c2, bonds[p]), (ct2, bonds[p].astype(F32).T.astype(BF16))):
            ref[p, :dof, :dof] = value
            ref[p, dof:, dof:] = value
            ref[p, :dof, dof:] = zero
            ref[p, dof:, :dof] = zero
    loads[7].wait()
    lax.fori_loop(0, half, build_own, 0)

    @pl.when(sp < 2)
    def _():
        q_in[...] = jnp.zeros_like(q_in)

    for load in loads[5:7]:
        load.wait()
    for i in range(1, n_x):
        b = 2 * ((x + n_x - i) % n_x) + core
        send_block(b, 0, sib).wait_recv()
        send_block(b, n_x + i, sib).start()
    for i in range(n_x):
        send_block(2 * ((x + n_x - i) % n_x) + 1 - core, 0, sib).wait_recv()

    def at_chunk(c):
        return pl.ds(pl.multiple_of(c * size, size), size)

    def s_copy(c):
        at = at_chunk(c)
        return copy(spec_out.at[:, at], spec.at[y, :, at], s_send.at[c], s_recv.at[c], span=peer)

    def transform(which, put):
        for case in range(0, cases, 2):
            value = jnp.concatenate(
                [gath[pl.ds(case + i, total, stride=cases), :] for i in range(2)], 1
            )
            high, low = split(value)
            result = dot(tf[which], jnp.concatenate([high, low, high], 0))
            for i in range(2):
                part = result[:, i * dof : (i + 1) * dof]
                put(0, pl.ds(case + i, half, stride=cases), part[:half])
                put(1, pl.ds(case + i, half, stride=cases), part[half:])

    def put_out(part, at, value):
        spec_out[part, at, :] = value

    def put_own(part, at, value):
        spec[y, part, at, :] = value

    transform(1 - y, put_out)
    for c in range(chunks):
        s_copy(c).start()
    transform(y, put_own)

    def f_copy(c):
        at = at_chunk(c)
        return copy(q_out.at[:, at], q_in.at[:, at], f_send.at[c], f_recv.at[c], span=sp + 2)

    def b_copy(c):
        at = at_chunk(c)
        return copy(solved.at[0, :, at], x_in.at[:, at], b_send.at[c], b_recv.at[c], span=sp - 2)

    def e_copy(c):
        at = at_chunk(c)
        return copy(
            solved.at[1 - y, :, at], other.at[:, at], e_send.at[c], e_recv.at[c], span=peer
        )

    def wide(ref, at):
        return jnp.concatenate([ref[0, at, :], ref[1, at, :]], 1)

    def put(ref, at, value):
        ref[0, at, :] = value[:, :dof]
        ref[1, at, :] = value[:, dof:]

    def times_pivots(value, p, c):
        high, low = split(value)
        parts = []
        for f in range(per):
            at = slice(f * cases, (f + 1) * cases)
            both = dot(jnp.concatenate([high[at], low[at]], 0), weights[p, c * per + f])
            parts.append(both[:cases] + both[cases:])
        return jnp.concatenate(parts, 0)

    def times_bond(value, bond):
        both = dot(jnp.concatenate(split(value), 0), bond)
        return both[:size] + both[size:]

    def finish(c, at, upper, lower):
        put(solved.at[1], at, upper)
        upper = lower - times_pivots(times_bond(upper, ct2[0]), 0, c)
        put(solved.at[0], at, upper)

        @pl.when(pair_below)
        def _():
            b_copy(c).start()

        e_copy(c).start()

    def up(c):
        at = at_chunk(c)
        p_copy(c).wait_recv()
        for f in range(per):
            build(1 - y, c * per + f)
        s_copy(c).wait_recv()

        @pl.when(pair_below)
        def _():
            f_copy(c).wait_recv()

        lower = times_pivots(wide(spec.at[0], at) - wide(q_in, at), 0, c)
        upper = times_pivots(wide(spec.at[1], at) - times_bond(lower, c2[0]), 1, c)

        @pl.when(pair_above)
        def _():
            put(q_out, at, times_bond(upper, c2[1]))
            f_copy(c).start()
            put(pv.at[0], at, lower)
            put(pv.at[1], at, upper)

        @pl.when(sp >= last - 1)
        def _():
            finish(c, at, upper, lower)

    def down(c):
        at = at_chunk(c)
        b_copy(c).wait_recv()
        upper = wide(pv.at[1], at) - times_pivots(times_bond(wide(x_in, at), ct2[1]), 1, c)
        finish(c, at, upper, wide(pv.at[0], at))

    lag = jnp.minimum(chunks, lead * ((last - sp) // 2))

    def turn(t, carry):
        @pl.when(t < chunks)
        def _():
            up(t)

        @pl.when(pair_above & (t >= lag) & (t < lag + chunks))
        def _():
            down(t - lag)

        return carry

    lax.fori_loop(0, 2 * chunks, turn, 0)
    for c in range(chunks):
        e_copy(c).wait_recv()

    def back(read, which, case):
        value = jnp.concatenate(
            [
                jnp.concatenate(
                    [read(p, pl.ds(case + i, half, stride=cases)) for p in range(2)], 0
                )
                for i in range(2)
            ],
            1,
        )
        high, low = split(value)
        return dot(ti[which], jnp.concatenate([high, low, high], 0))

    for case in range(0, cases, 2):
        result = back(lambda p, at: solved[y, p, at, :], y, case)
        result = result + back(lambda p, at: other[p, at, :], 1 - y, case)
        for i in range(2):
            contrib[pl.ds(case + i, total, stride=cases), :] = result[:, i * dof : (i + 1) * dof]

    def r1_copy(i):
        there = (x + i) % n_x
        return copy(
            contrib.at[block(2 * there + 1 - core)], rs1.at[i], r1_send.at[i], r1_recv.at[i], tm=sib
        )

    def r2_copy(i):
        there = (x + i) % n_x
        return copy(
            contrib.at[block(2 * there + core)], rs2.at[i], r2_send.at[i], r2_recv.at[i],
            tm=2 * there + core,
        )

    order = list(range(1, n_x)) + [0]
    for i in order:
        r1_copy(i).start()
    for i in order:
        r1_copy(i).wait_recv()
        at = block(2 * ((x + i) % n_x) + core)
        contrib[at] = contrib[at] + rs1[i]
        if i:
            r2_copy(i).start()
    result = contrib[mine] + iterate[...].astype(F32)
    for i in range(1, n_x):
        r2_copy(i).wait_recv()
        result = result + rs2[i]
    out[...] = result

    @pl.when(tm < n_tm - 1)
    def _():
        to_next.wait_send()

    @pl.when(has_above)
    def _():
        to_up.wait_send()
        c_up.wait_send()

    @pl.when(has_below)
    def _():
        to_down.wait_send()

    for slot in range(2 * n_x):
        if slot != n_x:
            send_block(tm, slot, sib).wait_send()

    for c in range(chunks):
        p_copy(c).wait_send()
        s_copy(c).wait_send()
        e_copy(c).wait_send()

    @pl.when(pair_above)
    def _():
        for c in range(chunks):
            f_copy(c).wait_send()

    @pl.when(pair_below)
    def _():
        for c in range(chunks):
            b_copy(c).wait_send()

    for i in range(n_x):
        r1_copy(i).wait_send()
    for i in range(1, n_x):
        r2_copy(i).wait_send()


def on_device(n_tm, n_sp, forcing, iterate, initial, stiffness, coupling, pivots):
    steps, planes, cases, dof = forcing.shape
    assert planes == 1 and n_tm % 2 == 0 and n_sp % 2 == 0 and steps % 2 == 0
    rows, total, n_x, half = steps * cases, steps * n_tm, n_tm // 2, steps // 2
    chunks = math.gcd(half, CHUNKS)
    forward, inverse = tables(total, n_tm)
    state = pltpu.VMEM((2, half * cases, dof), F32)
    both = pltpu.VMEM((2, 2, half * cases, dof), F32)
    dma = pltpu.SemaphoreType.DMA
    result = pl.pallas_call(
        functools.partial(kernel, n_tm, n_sp, chunks, LEAD, cases),
        out_shape=jax.ShapeDtypeStruct((rows, dof), F32),
        in_specs=[pl.BlockSpec(memory_space=pl.ANY)] * 8,
        out_specs=pl.BlockSpec(memory_space=pltpu.VMEM),
        scratch_shapes=[
            pltpu.VMEM((rows, dof), BF16),
            pltpu.VMEM((rows, dof), BF16),
            pltpu.VMEM((cases, dof), BF16),
            pltpu.VMEM((dof, dof), BF16),
            pltpu.VMEM((dof, dof), BF16),
            pltpu.VMEM((2, half, 2, dof, dof), BF16),
            pltpu.VMEM(forward.shape[1:], BF16),
            pltpu.VMEM(inverse.shape[1:], BF16),
            pltpu.VMEM((rows, dof), BF16),
            pltpu.VMEM((rows, dof), BF16),
            pltpu.VMEM((dof, dof), BF16),
            pltpu.VMEM((dof, dof), BF16),
            pltpu.VMEM((cases, dof), BF16),
            pltpu.VMEM((total * cases, dof), F32),
            pltpu.VMEM((2, half, 2 * dof, 2 * dof), BF16),
            pltpu.VMEM((2, 2 * dof, 2 * dof), BF16),
            pltpu.VMEM((2, 2 * dof, 2 * dof), BF16),
            both, state, both, state, state, state, both, state,
            pltpu.VMEM((total * cases, dof), F32),
            pltpu.VMEM((n_x, rows, dof), F32),
            pltpu.VMEM((n_x, rows, dof), F32),
            dma((8,)), dma((5,)), dma((5,)), dma((chunks,)), dma((chunks,)),
            dma((2 * n_x,)), dma((n_tm,)),
        ]
        + [dma((chunks,))] * 8
        + [dma((n_x,))] * 4,
        compiler_params=pltpu.CompilerParams(
            collective_id=0, has_side_effects=True, vmem_limit_bytes=60 * 2**20
        ),
    )(
        forcing.reshape(rows, dof),
        iterate.reshape(rows, dof),
        initial.reshape(cases, dof),
        stiffness.reshape(dof, dof),
        coupling.reshape(dof, dof),
        pivots.reshape(steps, 2, dof, dof),
        jnp.asarray(forward),
        jnp.asarray(inverse),
    )
    return result.reshape(steps, 1, cases, dof)


def solution(mesh):
    return jax.shard_map(
        functools.partial(on_device, mesh.shape["tm"], mesh.shape["span"]),
        mesh=mesh,
        in_specs=(
            P("tm", "span", None, None),
            P("tm", "span", None, None),
            P("span", None, None),
            P("span", None, None),
            P("span", None, None),
            P("tm", "span", None, None, None),
        ),
        out_specs=P("tm", "span", None, None),
        check_vma=False,
    )
```

```python
import functools
import math

import jax
import jax.numpy as jnp
import numpy as np
from jax import lax
from jax.experimental import pallas as pl
from jax.experimental.pallas import tpu as pltpu
from jax.sharding import PartitionSpec as P

MESH = pl.DeviceIdType.MESH
F32 = jnp.float32
CHUNKS = 8
LEAD = 8
EARLY = 5
BF16 = jnp.bfloat16


def split(value):
    high = value.astype(BF16)
    low = (value - high.astype(F32)).astype(BF16)
    return high, low


def dot(a, b):
    return jnp.dot(a, b, preferred_element_type=F32)


def tables(total, blocks):
    ids = np.arange(total)
    theta = 2.0 * math.pi / total * ((ids[:, None] * ids[None, :]) % total)
    gamma = 0.5 ** (ids / total)
    here = total // blocks

    def three(table):
        high = table.astype(np.float32).astype(jnp.bfloat16)
        low = (table - high.astype(np.float64)).astype(np.float32).astype(jnp.bfloat16)
        return np.concatenate([high, high, low], -1)

    half = here // 2
    cosine = (np.cos(theta) * gamma).reshape(blocks, 2, half, total)
    sine = (-np.sin(theta) * gamma).reshape(blocks, 2, half, total)
    forward = three(np.concatenate([cosine, sine], 2))
    back = 1.0 / (total * gamma[:, None])
    cosine = (np.cos(theta) * back).reshape(total, blocks, 2, half).transpose(1, 2, 0, 3)
    sine = (-np.sin(theta) * back).reshape(total, blocks, 2, half).transpose(1, 2, 0, 3)
    inverse = three(np.concatenate([cosine, sine], 3))
    return forward, inverse


def kernel(
    n_tm, n_sp, chunks, lead, cases, forcing_hbm, iterate_hbm, initial_hbm, stiff_hbm, coup_hbm,
    pivots_hbm, tf_hbm, ti_hbm, out,
    forcing, iterate, initial, stiff, coup, pivots, tf, ti,
    it_below, it_above, c_below, c_above, prior0, gath, weights, c2, ct2,
    spec, spec_out, pv, q_in, q_out, x_in, solved, other, contrib, rs1, rs2,
    ld, nb_send, nb_recv, p_send, p_recv, ag_send, ag_recv, s_send, s_recv,
    f_send, f_recv, b_send, b_recv, e_send, e_recv, r1_send, r1_recv, r2_send, r2_recv,
):
    tm, sp = lax.axis_index("tm"), lax.axis_index("span")
    rows, dof = iterate.shape
    steps = rows // cases
    total = steps * n_tm
    half = steps // 2
    per = half // chunks
    size = per * cases
    y = sp % 2
    peer = sp + 1 - 2 * y
    n_x = n_tm // 2
    core, x = tm % 2, tm // 2
    sib = 2 * x + 1 - core
    last = n_sp - 1
    has_below, has_above = sp > 0, sp < last
    pair_below, pair_above = sp > 1, sp < last - 1

    def copy(src, dst, send, recv, **where):
        return pltpu.make_async_remote_copy(
            src_ref=src, dst_ref=dst, send_sem=send, recv_sem=recv, device_id=where, device_id_type=MESH
        )

    loads = [
        pltpu.make_async_copy(src, dst, ld.at[i])
        for i, (src, dst) in enumerate(
            (
                (iterate_hbm, iterate),
                (stiff_hbm, stiff),
                (forcing_hbm, forcing),
                (initial_hbm, initial),
                (coup_hbm, coup),
                (tf_hbm.at[tm], tf),
                (ti_hbm.at[tm], ti),
                (pivots_hbm.at[pl.ds(y * half, half)], pivots.at[y]),
            )
        )
    ]
    for load in loads:
        load.start()

    def block(b):
        return pl.ds(pl.multiple_of(b * rows, rows), rows)

    barrier = pltpu.get_barrier_semaphore()
    for i in range(1, n_tm):
        pl.semaphore_signal(barrier, inc=1, device_id={"tm": (tm + i) % n_tm}, device_id_type=MESH)

    @pl.when(has_below)
    def _():
        pl.semaphore_signal(barrier, inc=1, device_id={"span": sp - 1}, device_id_type=MESH)

    @pl.when(has_above)
    def _():
        pl.semaphore_signal(barrier, inc=1, device_id={"span": sp + 1}, device_id_type=MESH)

    @pl.when(pair_below)
    def _():
        pl.semaphore_signal(barrier, inc=1, device_id={"span": sp - 2}, device_id_type=MESH)

    @pl.when(pair_above)
    def _():
        pl.semaphore_signal(barrier, inc=1, device_id={"span": sp + 2}, device_id_type=MESH)

    pl.semaphore_wait(
        barrier,
        n_tm - 1 + sum(t.astype(jnp.int32) for t in (has_below, has_above, pair_below, pair_above)),
    )

    to_up = copy(iterate_hbm, it_below, nb_send.at[0], nb_recv.at[0], span=sp + 1)
    to_down = copy(iterate_hbm, it_above, nb_send.at[1], nb_recv.at[1], span=sp - 1)
    c_up = copy(coup_hbm, c_below, nb_send.at[2], nb_recv.at[2], span=sp + 1)
    c_down = copy(coup_hbm, c_above, nb_send.at[4], nb_recv.at[4], span=sp - 1)
    on_up = copy(it_above, it_below, nb_send.at[5], nb_recv.at[5], span=sp + 2)
    on_down = copy(it_below, it_above, nb_send.at[6], nb_recv.at[6], span=sp - 2)
    c_on = copy(c_above, c_below, nb_send.at[7], nb_recv.at[7], span=sp + 2)
    to_next = copy(
        iterate_hbm.at[pl.ds(rows - cases, cases)], prior0, nb_send.at[3], nb_recv.at[3], tm=tm + 1
    )

    def p_copy(c):
        return copy(
            pivots_hbm.at[pl.ds((1 - y) * half + c * per, per)], pivots.at[y, pl.ds(c * per, per)],
            p_send.at[c], p_recv.at[c], span=peer,
        )

    @pl.when(tm < n_tm - 1)
    def _():
        to_next.start()

    @pl.when(y == 0)
    def _():
        to_up.start()
        c_up.start()

    @pl.when(y == 1)
    def _():
        to_down.start()
        c_down.start()

    early = min(EARLY, chunks)
    for c in range(early):
        p_copy(c).start()

    mine = block(tm)
    for load in loads[:5]:
        load.wait()
    it_wide = iterate[...].astype(F32)
    own = forcing[...].astype(F32) - it_wide - dot(iterate[...], stiff[...])
    own = own + jnp.concatenate([jnp.zeros((cases, dof), F32), it_wide[: rows - cases]], 0)
    gath[mine] = own
    first = pl.ds(pl.multiple_of(tm * rows, rows), cases)

    def build(p, k):
        real, imag = pivots[p, k, 0], pivots[p, k, 1]
        weights[p, k, :dof, :dof] = real
        weights[p, k, dof:, dof:] = real
        weights[p, k, :dof, dof:] = imag
        weights[p, k, dof:, :dof] = -imag

    def build_own(k, carry):
        build(y, k)
        return carry

    @pl.when(tm == 0)
    def _():
        gath[first] = gath[first] + initial[...].astype(F32)

    @pl.when(tm > 0)
    def _():
        to_next.wait_recv()
        gath[first] = gath[first] + prior0[...].astype(F32)

    @pl.when(y == 0)
    def _():
        to_down.wait_recv()
        c_down.wait_recv()

        @pl.when(pair_above)
        def _():
            on_up.start()
            c_on.start()

    @pl.when(y == 1)
    def _():
        to_up.wait_recv()
        c_up.wait_recv()

        @pl.when(pair_below)
        def _():
            on_down.start()

    def from_above():
        gath[mine] = gath[mine] - lax.dot_general(
            it_above[...], coup[...], (((1,), (1,)), ((), ())), preferred_element_type=F32
        )

    def from_below():
        gath[mine] = gath[mine] - dot(it_below[...], c_below[...])

    @pl.when(y == 0)
    def _():
        from_above()

        @pl.when(pair_below)
        def _():
            on_up.wait_recv()
            c_on.wait_recv()
            from_below()

    @pl.when(y == 1)
    def _():
        from_below()

        @pl.when(pair_above)
        def _():
            on_down.wait_recv()
            from_above()

    def send_block(b, slot, peer):
        at = block(b)
        return copy(gath.at[at], gath.at[at], ag_send.at[slot], ag_recv.at[b], tm=peer)

    for i in range(1, n_x):
        send_block(tm, i, 2 * ((x + i) % n_x) + core).start()
    send_block(tm, 0, sib).start()

    zero = jnp.zeros((dof, dof), BF16)
    bonds = (
        jnp.where(y == 0, coup[...], c_below[...]), jnp.where(y == 0, c_above[...], coup[...])
    )
    for p in range(2):
        for ref, value in ((c2, bonds[p]), (ct2, bonds[p].astype(F32).T.astype(BF16))):
            ref[p, :dof, :dof] = value
            ref[p, dof:, dof:] = value
            ref[p, :dof, dof:] = zero
            ref[p, dof:, :dof] = zero
    loads[7].wait()
    lax.fori_loop(0, half, build_own, 0)

    @pl.when(sp < 2)
    def _():
        q_in[...] = jnp.zeros_like(q_in)

    for load in loads[5:7]:
        load.wait()
    for i in range(1, n_x):
        b = 2 * ((x + n_x - i) % n_x) + core
        send_block(b, 0, sib).wait_recv()
        send_block(b, n_x + i, sib).start()
    for i in range(n_x):
        send_block(2 * ((x + n_x - i) % n_x) + 1 - core, 0, sib).wait_recv()

    def at_chunk(c):
        return pl.ds(pl.multiple_of(c * size, size), size)

    def s_copy(c):
        at = at_chunk(c)
        return copy(spec_out.at[:, at], spec.at[y, :, at], s_send.at[c], s_recv.at[c], span=peer)

    def transform(which, put):
        for case in range(0, cases, 2):
            value = jnp.concatenate(
                [gath[pl.ds(case + i, total, stride=cases), :] for i in range(2)], 1
            )
            high, low = split(value)
            result = dot(tf[which], jnp.concatenate([high, low, high], 0))
            for i in range(2):
                part = result[:, i * dof : (i + 1) * dof]
                put(0, pl.ds(case + i, half, stride=cases), part[:half])
                put(1, pl.ds(case + i, half, stride=cases), part[half:])

    def put_out(part, at, value):
        spec_out[part, at, :] = value

    def put_own(part, at, value):
        spec[y, part, at, :] = value

    transform(1 - y, put_out)
    for c in range(chunks):
        s_copy(c).start()
    for c in range(early, chunks):
        p_copy(c).start()
    transform(y, put_own)

    def f_copy(c):
        at = at_chunk(c)
        return copy(q_out.at[:, at], q_in.at[:, at], f_send.at[c], f_recv.at[c], span=sp + 2)

    def b_copy(c):
        at = at_chunk(c)
        return copy(solved.at[0, :, at], x_in.at[:, at], b_send.at[c], b_recv.at[c], span=sp - 2)

    def e_copy(c):
        at = at_chunk(c)
        return copy(
            solved.at[1 - y, :, at], other.at[:, at], e_send.at[c], e_recv.at[c], span=peer
        )

    def wide(ref, at):
        return jnp.concatenate([ref[0, at, :], ref[1, at, :]], 1)

    def put(ref, at, value):
        ref[0, at, :] = value[:, :dof]
        ref[1, at, :] = value[:, dof:]

    def times_pivots(value, p, c):
        high, low = split(value)
        parts = []
        for f in range(per):
            at = slice(f * cases, (f + 1) * cases)
            both = dot(jnp.concatenate([high[at], low[at]], 0), weights[p, c * per + f])
            parts.append(both[:cases] + both[cases:])
        return jnp.concatenate(parts, 0)

    def times_bond(value, bond):
        both = dot(jnp.concatenate(split(value), 0), bond)
        return both[:size] + both[size:]

    def finish(c, at, upper, lower):
        put(solved.at[1], at, upper)
        upper = lower - times_pivots(times_bond(upper, ct2[0]), 0, c)
        put(solved.at[0], at, upper)

        @pl.when(pair_below)
        def _():
            b_copy(c).start()

        e_copy(c).start()

    def up(c):
        at = at_chunk(c)
        p_copy(c).wait_recv()
        for f in range(per):
            build(1 - y, c * per + f)
        s_copy(c).wait_recv()

        @pl.when(pair_below)
        def _():
            f_copy(c).wait_recv()

        lower = times_pivots(wide(spec.at[0], at) - wide(q_in, at), 0, c)
        upper = times_pivots(wide(spec.at[1], at) - times_bond(lower, c2[0]), 1, c)

        @pl.when(pair_above)
        def _():
            put(q_out, at, times_bond(upper, c2[1]))
            f_copy(c).start()
            put(pv.at[0], at, lower)
            put(pv.at[1], at, upper)

        @pl.when(sp >= last - 1)
        def _():
            finish(c, at, upper, lower)

    def down(c):
        at = at_chunk(c)
        b_copy(c).wait_recv()
        upper = wide(pv.at[1], at) - times_pivots(times_bond(wide(x_in, at), ct2[1]), 1, c)
        finish(c, at, upper, wide(pv.at[0], at))

    lag = jnp.minimum(chunks, lead * ((last - sp) // 2))

    def turn(t, carry):
        @pl.when(t < chunks)
        def _():
            up(t)

        @pl.when(pair_above & (t >= lag) & (t < lag + chunks))
        def _():
            down(t - lag)

        return carry

    lax.fori_loop(0, 2 * chunks, turn, 0)
    for c in range(chunks):
        e_copy(c).wait_recv()

    def back(read, which, case):
        value = jnp.concatenate(
            [
                jnp.concatenate(
                    [read(p, pl.ds(case + i, half, stride=cases)) for p in range(2)], 0
                )
                for i in range(2)
            ],
            1,
        )
        high, low = split(value)
        return dot(ti[which], jnp.concatenate([high, low, high], 0))

    for case in range(0, cases, 2):
        result = back(lambda p, at: solved[y, p, at, :], y, case)
        result = result + back(lambda p, at: other[p, at, :], 1 - y, case)
        for i in range(2):
            contrib[pl.ds(case + i, total, stride=cases), :] = result[:, i * dof : (i + 1) * dof]

    def r1_copy(i):
        there = (x + i) % n_x
        return copy(
            contrib.at[block(2 * there + 1 - core)], rs1.at[i], r1_send.at[i], r1_recv.at[i], tm=sib
        )

    def r2_copy(i):
        there = (x + i) % n_x
        return copy(
            contrib.at[block(2 * there + core)], rs2.at[i], r2_send.at[i], r2_recv.at[i],
            tm=2 * there + core,
        )

    order = list(range(1, n_x)) + [0]
    for i in order:
        r1_copy(i).start()
    for i in order:
        r1_copy(i).wait_recv()
        at = block(2 * ((x + i) % n_x) + core)
        contrib[at] = contrib[at] + rs1[i]
        if i:
            r2_copy(i).start()
    result = contrib[mine] + iterate[...].astype(F32)
    for i in range(1, n_x):
        r2_copy(i).wait_recv()
        result = result + rs2[i]
    out[...] = result

    @pl.when(tm < n_tm - 1)
    def _():
        to_next.wait_send()

    @pl.when(y == 0)
    def _():
        to_up.wait_send()
        c_up.wait_send()

        @pl.when(pair_above)
        def _():
            on_up.wait_send()
            c_on.wait_send()

    @pl.when(y == 1)
    def _():
        to_down.wait_send()
        c_down.wait_send()

        @pl.when(pair_below)
        def _():
            on_down.wait_send()

    for slot in range(2 * n_x):
        if slot != n_x:
            send_block(tm, slot, sib).wait_send()

    for c in range(chunks):
        p_copy(c).wait_send()
        s_copy(c).wait_send()
        e_copy(c).wait_send()

    @pl.when(pair_above)
    def _():
        for c in range(chunks):
            f_copy(c).wait_send()

    @pl.when(pair_below)
    def _():
        for c in range(chunks):
            b_copy(c).wait_send()

    for i in range(n_x):
        r1_copy(i).wait_send()
    for i in range(1, n_x):
        r2_copy(i).wait_send()


def on_device(n_tm, n_sp, forcing, iterate, initial, stiffness, coupling, pivots):
    steps, planes, cases, dof = forcing.shape
    assert planes == 1 and n_tm % 2 == 0 and n_sp % 2 == 0 and steps % 2 == 0
    rows, total, n_x, half = steps * cases, steps * n_tm, n_tm // 2, steps // 2
    chunks = math.gcd(half, CHUNKS)
    forward, inverse = tables(total, n_tm)
    state = pltpu.VMEM((2, half * cases, dof), F32)
    both = pltpu.VMEM((2, 2, half * cases, dof), F32)
    dma = pltpu.SemaphoreType.DMA
    result = pl.pallas_call(
        functools.partial(kernel, n_tm, n_sp, chunks, LEAD, cases),
        out_shape=jax.ShapeDtypeStruct((rows, dof), F32),
        in_specs=[pl.BlockSpec(memory_space=pl.ANY)] * 8,
        out_specs=pl.BlockSpec(memory_space=pltpu.VMEM),
        scratch_shapes=[
            pltpu.VMEM((rows, dof), BF16),
            pltpu.VMEM((rows, dof), BF16),
            pltpu.VMEM((cases, dof), BF16),
            pltpu.VMEM((dof, dof), BF16),
            pltpu.VMEM((dof, dof), BF16),
            pltpu.VMEM((2, half, 2, dof, dof), BF16),
            pltpu.VMEM(forward.shape[1:], BF16),
            pltpu.VMEM(inverse.shape[1:], BF16),
            pltpu.VMEM((rows, dof), BF16),
            pltpu.VMEM((rows, dof), BF16),
            pltpu.VMEM((dof, dof), BF16),
            pltpu.VMEM((dof, dof), BF16),
            pltpu.VMEM((cases, dof), BF16),
            pltpu.VMEM((total * cases, dof), F32),
            pltpu.VMEM((2, half, 2 * dof, 2 * dof), BF16),
            pltpu.VMEM((2, 2 * dof, 2 * dof), BF16),
            pltpu.VMEM((2, 2 * dof, 2 * dof), BF16),
            both, state, both, state, state, state, both, state,
            pltpu.VMEM((total * cases, dof), F32),
            pltpu.VMEM((n_x, rows, dof), F32),
            pltpu.VMEM((n_x, rows, dof), F32),
            dma((8,)), dma((8,)), dma((8,)), dma((chunks,)), dma((chunks,)),
            dma((2 * n_x,)), dma((n_tm,)),
        ]
        + [dma((chunks,))] * 8
        + [dma((n_x,))] * 4,
        compiler_params=pltpu.CompilerParams(
            collective_id=0, has_side_effects=True, vmem_limit_bytes=60 * 2**20
        ),
    )(
        forcing.reshape(rows, dof),
        iterate.reshape(rows, dof),
        initial.reshape(cases, dof),
        stiffness.reshape(dof, dof),
        coupling.reshape(dof, dof),
        pivots.reshape(steps, 2, dof, dof),
        jnp.asarray(forward),
        jnp.asarray(inverse),
    )
    return result.reshape(steps, 1, cases, dof)


def solution(mesh):
    return jax.shard_map(
        functools.partial(on_device, mesh.shape["tm"], mesh.shape["span"]),
        mesh=mesh,
        in_specs=(
            P("tm", "span", None, None),
            P("tm", "span", None, None),
            P("span", None, None),
            P("span", None, None),
            P("span", None, None),
            P("tm", "span", None, None, None),
        ),
        out_specs=P("tm", "span", None, None),
        check_vma=False,
    )
```

```python
import functools
import math

import jax
import jax.numpy as jnp
import numpy as np
from jax import lax
from jax.experimental import pallas as pl
from jax.experimental.pallas import tpu as pltpu
from jax.sharding import PartitionSpec as P

MESH = pl.DeviceIdType.MESH
F32 = jnp.float32
CHUNKS = 8
LEAD = 8
EARLY = 5
BF16 = jnp.bfloat16


def split(value):
    high = value.astype(BF16)
    low = (value - high.astype(F32)).astype(BF16)
    return high, low


def dot(a, b):
    return jnp.dot(a, b, preferred_element_type=F32)


def tables(total, blocks):
    ids = np.arange(total)
    theta = 2.0 * math.pi / total * ((ids[:, None] * ids[None, :]) % total)
    gamma = 0.5 ** (ids / total)
    here = total // blocks

    def three(table):
        high = table.astype(np.float32).astype(jnp.bfloat16)
        low = (table - high.astype(np.float64)).astype(np.float32).astype(jnp.bfloat16)
        return np.concatenate([high, high, low], -1)

    half = here // 2
    cosine = (np.cos(theta) * gamma).reshape(blocks, 2, half, total)
    sine = (-np.sin(theta) * gamma).reshape(blocks, 2, half, total)
    forward = three(np.concatenate([cosine, sine], 2))
    back = 1.0 / (total * gamma[:, None])
    cosine = (np.cos(theta) * back).reshape(total, blocks, 2, half).transpose(1, 2, 0, 3)
    sine = (-np.sin(theta) * back).reshape(total, blocks, 2, half).transpose(1, 2, 0, 3)
    inverse = three(np.concatenate([cosine, sine], 3))
    return forward, inverse


def kernel(
    n_tm, n_sp, chunks, lead, cases, forcing_hbm, iterate_hbm, initial_hbm, stiff_hbm, coup_hbm,
    pivots_hbm, tf_hbm, ti_hbm, out,
    forcing, iterate, initial, stiff, coup, pivots, tf, ti,
    it_below, it_above, c_below, c_above, prior0, gath, weights, c2, ct2,
    spec, spec_out, pv, q_in, q_out, x_in, solved, other, contrib, rs1, rs2,
    ld, nb_send, nb_recv, p_send, p_recv, ag_send, ag_recv, s_send, s_recv,
    f_send, f_recv, b_send, b_recv, e_send, e_recv, r1_send, r1_recv, r2_send, r2_recv,
):
    tm, sp = lax.axis_index("tm"), lax.axis_index("span")
    rows, dof = iterate.shape
    steps = rows // cases
    total = steps * n_tm
    half = steps // 2
    per = half // chunks
    size = per * cases
    y = sp % 2
    peer = sp + 1 - 2 * y
    n_x = n_tm // 2
    core, x = tm % 2, tm // 2
    sib = 2 * x + 1 - core
    last = n_sp - 1
    has_below, has_above = sp > 0, sp < last
    pair_below, pair_above = sp > 1, sp < last - 1

    def copy(src, dst, send, recv, **where):
        return pltpu.make_async_remote_copy(
            src_ref=src, dst_ref=dst, send_sem=send, recv_sem=recv, device_id=where, device_id_type=MESH
        )

    loads = [
        pltpu.make_async_copy(src, dst, ld.at[i])
        for i, (src, dst) in enumerate(
            (
                (iterate_hbm, iterate),
                (stiff_hbm, stiff),
                (forcing_hbm, forcing),
                (initial_hbm, initial),
                (coup_hbm, coup),
                (tf_hbm.at[tm], tf),
                (ti_hbm.at[tm], ti),
                (pivots_hbm.at[pl.ds(y * half, half)], pivots.at[y]),
            )
        )
    ]
    for load in loads:
        load.start()

    def block(b):
        return pl.ds(pl.multiple_of(b * rows, rows), rows)

    barrier = pltpu.get_barrier_semaphore()
    for i in range(1, n_tm):
        pl.semaphore_signal(barrier, inc=1, device_id={"tm": (tm + i) % n_tm}, device_id_type=MESH)

    @pl.when(has_below)
    def _():
        pl.semaphore_signal(barrier, inc=1, device_id={"span": sp - 1}, device_id_type=MESH)

    @pl.when(has_above)
    def _():
        pl.semaphore_signal(barrier, inc=1, device_id={"span": sp + 1}, device_id_type=MESH)

    @pl.when(pair_below)
    def _():
        pl.semaphore_signal(barrier, inc=1, device_id={"span": sp - 2}, device_id_type=MESH)

    @pl.when(pair_above)
    def _():
        pl.semaphore_signal(barrier, inc=1, device_id={"span": sp + 2}, device_id_type=MESH)

    pl.semaphore_wait(
        barrier,
        n_tm - 1 + sum(t.astype(jnp.int32) for t in (has_below, has_above, pair_below, pair_above)),
    )

    to_up = copy(iterate_hbm, it_below, nb_send.at[0], nb_recv.at[0], span=sp + 1)
    to_down = copy(iterate_hbm, it_above, nb_send.at[1], nb_recv.at[1], span=sp - 1)
    c_up = copy(coup_hbm, c_below, nb_send.at[2], nb_recv.at[2], span=sp + 1)
    c_down = copy(coup_hbm, c_above, nb_send.at[4], nb_recv.at[4], span=sp - 1)
    on_up = copy(it_above, it_below, nb_send.at[5], nb_recv.at[5], span=sp + 2)
    on_down = copy(it_below, it_above, nb_send.at[6], nb_recv.at[6], span=sp - 2)
    c_on = copy(c_above, c_below, nb_send.at[7], nb_recv.at[7], span=sp + 2)
    to_next = copy(
        iterate_hbm.at[pl.ds(rows - cases, cases)], prior0, nb_send.at[3], nb_recv.at[3], tm=tm + 1
    )

    def p_copy(c):
        return copy(
            pivots_hbm.at[pl.ds((1 - y) * half + c * per, per)], pivots.at[y, pl.ds(c * per, per)],
            p_send.at[c], p_recv.at[c], span=peer,
        )

    @pl.when(tm < n_tm - 1)
    def _():
        to_next.start()

    @pl.when(y == 0)
    def _():
        to_up.start()
        c_up.start()

    @pl.when(y == 1)
    def _():
        to_down.start()
        c_down.start()

    early = min(EARLY, chunks)
    for c in range(early):
        p_copy(c).start()

    mine = block(tm)
    for load in loads[:5]:
        load.wait()
    it_wide = iterate[...].astype(F32)
    own = forcing[...].astype(F32) - it_wide - dot(iterate[...], stiff[...])
    own = own + jnp.concatenate([jnp.zeros((cases, dof), F32), it_wide[: rows - cases]], 0)
    gath[mine] = own
    first = pl.ds(pl.multiple_of(tm * rows, rows), cases)

    def build(p, k):
        real, imag = pivots[p, k, 0], pivots[p, k, 1]
        weights[p, k, :dof, :dof] = real
        weights[p, k, dof:, dof:] = real
        weights[p, k, :dof, dof:] = imag
        weights[p, k, dof:, :dof] = -imag

    def build_own(k, carry):
        build(y, k)
        return carry

    @pl.when(tm == 0)
    def _():
        gath[first] = gath[first] + initial[...].astype(F32)

    @pl.when(tm > 0)
    def _():
        to_next.wait_recv()
        gath[first] = gath[first] + prior0[...].astype(F32)

    @pl.when(y == 0)
    def _():
        to_down.wait_recv()
        c_down.wait_recv()

        @pl.when(pair_above)
        def _():
            on_up.start()
            c_on.start()

    @pl.when(y == 1)
    def _():
        to_up.wait_recv()
        c_up.wait_recv()

        @pl.when(pair_below)
        def _():
            on_down.start()

    def from_above():
        gath[mine] = gath[mine] - lax.dot_general(
            it_above[...], coup[...], (((1,), (1,)), ((), ())), preferred_element_type=F32
        )

    def from_below():
        gath[mine] = gath[mine] - dot(it_below[...], c_below[...])

    @pl.when(y == 0)
    def _():
        from_above()

        @pl.when(pair_below)
        def _():
            on_up.wait_recv()
            c_on.wait_recv()
            from_below()

    @pl.when(y == 1)
    def _():
        from_below()

        @pl.when(pair_above)
        def _():
            on_down.wait_recv()
            from_above()

    def send_block(b, slot, peer):
        at = block(b)
        return copy(gath.at[at], gath.at[at], ag_send.at[slot], ag_recv.at[b], tm=peer)

    for i in range(1, n_x):
        send_block(tm, i, 2 * ((x + i) % n_x) + core).start()
    send_block(tm, 0, sib).start()

    zero = jnp.zeros((dof, dof), BF16)
    bonds = (
        jnp.where(y == 0, coup[...], c_below[...]), jnp.where(y == 0, c_above[...], coup[...])
    )
    for p in range(2):
        for ref, value in ((c2, bonds[p]), (ct2, bonds[p].astype(F32).T.astype(BF16))):
            ref[p, :dof, :dof] = value
            ref[p, dof:, dof:] = value
            ref[p, :dof, dof:] = zero
            ref[p, dof:, :dof] = zero
    loads[7].wait()
    lax.fori_loop(0, half, build_own, 0)

    @pl.when(sp < 2)
    def _():
        q_in[...] = jnp.zeros_like(q_in)

    for load in loads[5:7]:
        load.wait()
    for i in range(1, n_x):
        b = 2 * ((x + n_x - i) % n_x) + core
        send_block(b, 0, sib).wait_recv()
        send_block(b, n_x + i, sib).start()
    for i in range(n_x):
        send_block(2 * ((x + n_x - i) % n_x) + 1 - core, 0, sib).wait_recv()

    def at_chunk(c):
        return pl.ds(pl.multiple_of(c * size, size), size)

    def s_copy(c):
        at = at_chunk(c)
        return copy(spec_out.at[:, at], spec.at[y, :, at], s_send.at[c], s_recv.at[c], span=peer)

    def transform(which, put):
        for case in range(0, cases, 2):
            value = jnp.concatenate(
                [gath[pl.ds(case + i, total, stride=cases), :] for i in range(2)], 1
            )
            high, low = split(value)
            result = dot(tf[which], jnp.concatenate([high, low, high], 0))
            for i in range(2):
                part = result[:, i * dof : (i + 1) * dof]
                put(0, pl.ds(case + i, half, stride=cases), part[:half])
                put(1, pl.ds(case + i, half, stride=cases), part[half:])

    def put_out(part, at, value):
        spec_out[part, at, :] = value

    def put_own(part, at, value):
        spec[y, part, at, :] = value

    transform(1 - y, put_out)
    for c in range(chunks):
        s_copy(c).start()
    for c in range(early, chunks):
        p_copy(c).start()
    transform(y, put_own)

    def f_copy(c):
        at = at_chunk(c)
        return copy(q_out.at[:, at], q_in.at[:, at], f_send.at[c], f_recv.at[c], span=sp + 2)

    def b_copy(c):
        at = at_chunk(c)
        return copy(solved.at[0, :, at], x_in.at[:, at], b_send.at[c], b_recv.at[c], span=sp - 2)

    def e_copy(c):
        at = at_chunk(c)
        return copy(
            solved.at[1 - y, :, at], other.at[:, at], e_send.at[c], e_recv.at[c], span=peer
        )

    def wide(ref, at):
        return jnp.concatenate([ref[0, at, :], ref[1, at, :]], 1)

    def put(ref, at, value):
        ref[0, at, :] = value[:, :dof]
        ref[1, at, :] = value[:, dof:]

    def times_pivots(value, p, c):
        high, low = split(value)
        parts = []
        for f in range(per):
            at = slice(f * cases, (f + 1) * cases)
            both = dot(jnp.concatenate([high[at], low[at]], 0), weights[p, c * per + f])
            parts.append(both[:cases] + both[cases:])
        return jnp.concatenate(parts, 0)

    def times_bond(value, bond):
        both = dot(jnp.concatenate(split(value), 0), bond)
        return both[:size] + both[size:]

    def finish(c, at, upper, lower):
        put(solved.at[1], at, upper)
        upper = lower - times_pivots(times_bond(upper, ct2[0]), 0, c)
        put(solved.at[0], at, upper)

        @pl.when(pair_below)
        def _():
            b_copy(c).start()

        e_copy(c).start()

    def up(c):
        at = at_chunk(c)
        p_copy(c).wait_recv()
        for f in range(per):
            build(1 - y, c * per + f)
        s_copy(c).wait_recv()

        @pl.when(pair_below)
        def _():
            f_copy(c).wait_recv()

        lower = times_pivots(wide(spec.at[0], at) - wide(q_in, at), 0, c)
        upper = times_pivots(wide(spec.at[1], at) - times_bond(lower, c2[0]), 1, c)

        @pl.when(pair_above)
        def _():
            put(q_out, at, times_bond(upper, c2[1]))
            f_copy(c).start()
            put(pv.at[0], at, lower)
            put(pv.at[1], at, upper)

        @pl.when(sp >= last - 1)
        def _():
            finish(c, at, upper, lower)

    def down(c):
        at = at_chunk(c)
        b_copy(c).wait_recv()
        upper = wide(pv.at[1], at) - times_pivots(times_bond(wide(x_in, at), ct2[1]), 1, c)
        finish(c, at, upper, wide(pv.at[0], at))

    lag = jnp.minimum(chunks, lead * ((last - sp) // 2))

    def turn(t, carry):
        @pl.when(t < chunks)
        def _():
            up(t)

        @pl.when(pair_above & (t >= lag) & (t < lag + chunks))
        def _():
            down(t - lag)

        return carry

    lax.fori_loop(0, 2 * chunks, turn, 0)
    def back(read, which, case):
        value = jnp.concatenate(
            [
                jnp.concatenate(
                    [read(p, pl.ds(case + i, half, stride=cases)) for p in range(2)], 0
                )
                for i in range(2)
            ],
            1,
        )
        high, low = split(value)
        return dot(ti[which], jnp.concatenate([high, low, high], 0))

    for case in range(0, cases, 2):
        result = back(lambda p, at: solved[y, p, at, :], y, case)
        for i in range(2):
            contrib[pl.ds(case + i, total, stride=cases), :] = result[:, i * dof : (i + 1) * dof]
    for c in range(chunks):
        e_copy(c).wait_recv()
    for case in range(0, cases, 2):
        result = back(lambda p, at: other[p, at, :], 1 - y, case)
        for i in range(2):
            at = pl.ds(case + i, total, stride=cases)
            contrib[at, :] = contrib[at, :] + result[:, i * dof : (i + 1) * dof]

    def r1_copy(i):
        there = (x + i) % n_x
        return copy(
            contrib.at[block(2 * there + 1 - core)], rs1.at[i], r1_send.at[i], r1_recv.at[i], tm=sib
        )

    def r2_copy(i):
        there = (x + i) % n_x
        return copy(
            contrib.at[block(2 * there + core)], rs2.at[i], r2_send.at[i], r2_recv.at[i],
            tm=2 * there + core,
        )

    order = list(range(1, n_x)) + [0]
    for i in order:
        r1_copy(i).start()
    for i in order:
        r1_copy(i).wait_recv()
        at = block(2 * ((x + i) % n_x) + core)
        contrib[at] = contrib[at] + rs1[i]
        if i:
            r2_copy(i).start()
    result = contrib[mine] + iterate[...].astype(F32)
    for i in range(1, n_x):
        r2_copy(i).wait_recv()
        result = result + rs2[i]
    out[...] = result

    @pl.when(tm < n_tm - 1)
    def _():
        to_next.wait_send()

    @pl.when(y == 0)
    def _():
        to_up.wait_send()
        c_up.wait_send()

        @pl.when(pair_above)
        def _():
            on_up.wait_send()
            c_on.wait_send()

    @pl.when(y == 1)
    def _():
        to_down.wait_send()
        c_down.wait_send()

        @pl.when(pair_below)
        def _():
            on_down.wait_send()

    for slot in range(2 * n_x):
        if slot != n_x:
            send_block(tm, slot, sib).wait_send()

    for c in range(chunks):
        p_copy(c).wait_send()
        s_copy(c).wait_send()
        e_copy(c).wait_send()

    @pl.when(pair_above)
    def _():
        for c in range(chunks):
            f_copy(c).wait_send()

    @pl.when(pair_below)
    def _():
        for c in range(chunks):
            b_copy(c).wait_send()

    for i in range(n_x):
        r1_copy(i).wait_send()
    for i in range(1, n_x):
        r2_copy(i).wait_send()


def on_device(n_tm, n_sp, forcing, iterate, initial, stiffness, coupling, pivots):
    steps, planes, cases, dof = forcing.shape
    assert planes == 1 and n_tm % 2 == 0 and n_sp % 2 == 0 and steps % 2 == 0
    rows, total, n_x, half = steps * cases, steps * n_tm, n_tm // 2, steps // 2
    chunks = math.gcd(half, CHUNKS)
    forward, inverse = tables(total, n_tm)
    state = pltpu.VMEM((2, half * cases, dof), F32)
    both = pltpu.VMEM((2, 2, half * cases, dof), F32)
    dma = pltpu.SemaphoreType.DMA
    result = pl.pallas_call(
        functools.partial(kernel, n_tm, n_sp, chunks, LEAD, cases),
        out_shape=jax.ShapeDtypeStruct((rows, dof), F32),
        in_specs=[pl.BlockSpec(memory_space=pl.ANY)] * 8,
        out_specs=pl.BlockSpec(memory_space=pltpu.VMEM),
        scratch_shapes=[
            pltpu.VMEM((rows, dof), BF16),
            pltpu.VMEM((rows, dof), BF16),
            pltpu.VMEM((cases, dof), BF16),
            pltpu.VMEM((dof, dof), BF16),
            pltpu.VMEM((dof, dof), BF16),
            pltpu.VMEM((2, half, 2, dof, dof), BF16),
            pltpu.VMEM(forward.shape[1:], BF16),
            pltpu.VMEM(inverse.shape[1:], BF16),
            pltpu.VMEM((rows, dof), BF16),
            pltpu.VMEM((rows, dof), BF16),
            pltpu.VMEM((dof, dof), BF16),
            pltpu.VMEM((dof, dof), BF16),
            pltpu.VMEM((cases, dof), BF16),
            pltpu.VMEM((total * cases, dof), F32),
            pltpu.VMEM((2, half, 2 * dof, 2 * dof), BF16),
            pltpu.VMEM((2, 2 * dof, 2 * dof), BF16),
            pltpu.VMEM((2, 2 * dof, 2 * dof), BF16),
            both, state, both, state, state, state, both, state,
            pltpu.VMEM((total * cases, dof), F32),
            pltpu.VMEM((n_x, rows, dof), F32),
            pltpu.VMEM((n_x, rows, dof), F32),
            dma((8,)), dma((8,)), dma((8,)), dma((chunks,)), dma((chunks,)),
            dma((2 * n_x,)), dma((n_tm,)),
        ]
        + [dma((chunks,))] * 8
        + [dma((n_x,))] * 4,
        compiler_params=pltpu.CompilerParams(
            collective_id=0, has_side_effects=True, vmem_limit_bytes=60 * 2**20
        ),
    )(
        forcing.reshape(rows, dof),
        iterate.reshape(rows, dof),
        initial.reshape(cases, dof),
        stiffness.reshape(dof, dof),
        coupling.reshape(dof, dof),
        pivots.reshape(steps, 2, dof, dof),
        jnp.asarray(forward),
        jnp.asarray(inverse),
    )
    return result.reshape(steps, 1, cases, dof)


def solution(mesh):
    return jax.shard_map(
        functools.partial(on_device, mesh.shape["tm"], mesh.shape["span"]),
        mesh=mesh,
        in_specs=(
            P("tm", "span", None, None),
            P("tm", "span", None, None),
            P("span", None, None),
            P("span", None, None),
            P("span", None, None),
            P("tm", "span", None, None, None),
        ),
        out_specs=P("tm", "span", None, None),
        check_vma=False,
    )
```
